32 devices in a mesh: groups: 2 (over y), dp: 4 (over z), tensor: 4 (over x, core).
Axes of the slice: x: 2, y: 2, z: 4, core: 2. Of those that a mesh axis runs over, the one named last changes fastest.
Arguments:
- ssm_input: bfloat16 [8, 512, 8192], P(('groups', 'dp'), None, 'tensor'), parts along dimension 0, may hold values from -6 to 6
- input_proj: bfloat16 [8, 512, 512], P(('groups', 'dp'), None, 'tensor'), parts along dimension 0, may hold values from -2 to 2
- output_proj: bfloat16 [8, 512, 512], P(('groups', 'dp'), None, 'tensor'), parts along dimension 0, may hold values from -2 to 2
- step_raw: float32 [8, 128, 512], P(('groups', 'dp'), 'tensor'), parts along dimension 0, may hold values from -4 to 4
- step_bias: float32 [128], P('tensor'), may hold values from -1 to 1
- decay_log: float32 [128], P('tensor'), may hold values from -5.8 to -2.8
- skip_gain: float32 [128], P('tensor'), may hold values from 0.5 to 1.5
- norm_gain: float32 [8192], P('tensor'), may hold values from 0.1 to 1.9
- cache_states: bfloat16 [32, 128, 64, 128], P('groups', 'tensor', 'dp'), parts along dimension 0, may hold values from -6 to 6
- slot_decay: float32 [32, 128], P('groups', 'tensor'), parts along dimension 0, may hold values from 0.2 to 0.9
- template_state: bfloat16 [256, 64, 128], P(('groups', 'tensor'), 'dp'), parts along dimension 0, may hold values from -6 to 6
- slot_ids: int32 [8], P(('groups', 'dp')), parts along dimension 0, may hold values from 0 to 15
- row_lengths: int32 [8], P(('groups', 'dp')), parts along dimension 0, may hold values from 256 to 512
- row_offsets: int32 [8], P(('groups', 'dp')), parts along dimension 0, may hold values from 0 to 127
Outputs:
- mixed: bfloat16 [8, 512, 8192], P(('groups', 'dp'), None, 'tensor'), parts along dimension 0
- new_states: bfloat16 [8, 128, 64, 128], P('groups', 'tensor', 'dp'), parts along dimension 0
The draws below stay inside these ranges and needn't reach their ends.
There are 2 independent parts, one for each index of `groups`. The reference program is written for one: setup_inputs(seed, part) draws one part's arguments, and reference() takes and returns one part's arrays. A program takes and returns all parts, laid end to end along the dimension named above; an argument that names none is the same for every part. Nothing has to cross between parts.
All inputs are finite; a program needn't handle non-finite values.
Results may differ from the reference program's by a relative error of at most 0.0049.
Values may be sent and summed in bfloat16 or wider, within the bound.
No kernel may reach another device: no remote copies, remote signals or barrier semaphores. Data moves between devices by JAX's collectives and lax.ppermute only.
A program may use at most 64 MiB of HBM per device.

```python
import jax
import jax.numpy as jnp
from jax import lax

HEAD_SIZE = 64
STATE_SIZE = 128
GROUP_HEADS = 32
HEADS = 128
GROUPS = 4
TOKENS_ROW = 512
ROWS = 4
SLOTS = 16


def touch_ends(result, key, low, high):
    longest = result.shape.index(max(result.shape))
    spots = []
    for shift in (0, 1):
        where = [jax.random.randint(jax.random.fold_in(key, axis), (), 0, length) for axis, length in enumerate(result.shape)]
        where[longest] = (where[longest] + shift) % result.shape[longest]
        spots.append(tuple(where))
    return result.at[spots[0]].set(low).at[spots[1]].set(high)


def level_of(rng, dims, split, low, high):
    gain, own = 1.0, jax.random.fold_in(rng, 6)
    for dim, blocks in split:
        draws = jnp.exp(jax.random.uniform(jax.random.fold_in(own, dim), (blocks,), jnp.float32, low / len(split), high / len(split)))
        gain = gain * jnp.repeat(draws, dims[dim] // blocks).reshape([-1 if axis == dim else 1 for axis in range(len(dims))])
    return gain


def gaussian(stream_key, extent, scale, bound, shards=(), held_as=jnp.bfloat16):
    loudness = level_of(stream_key, extent, shards, -0.22, 0.18) if shards else 1.0
    entries = jax.random.normal(stream_key, extent, jnp.float32) * scale * loudness
    return jnp.minimum(jnp.maximum(entries, -bound), bound).astype(held_as)


def setup_inputs(seed: int = 0, part: int = 0) -> dict:
    keys = jax.random.split(jax.random.key(seed), 15)
    part_splits = jax.random.split(jax.random.fold_in(keys[14], part), 15)
    return {
        "ssm_input": gaussian(part_splits[0], (ROWS, TOKENS_ROW, HEADS * HEAD_SIZE), 1.0, 6.0, ((0, 4), (2, 4))),
        "input_proj": gaussian(part_splits[1], (ROWS, TOKENS_ROW, GROUPS * STATE_SIZE), 0.3, 2.0, ((0, 4), (2, 4))),
        "output_proj": gaussian(part_splits[2], (ROWS, TOKENS_ROW, GROUPS * STATE_SIZE), 0.3, 2.0, ((0, 4), (2, 4))),
        "step_raw": gaussian(part_splits[3], (ROWS, HEADS, TOKENS_ROW), 0.7, 4.0, ((0, 4), (1, 4)), jnp.float32),
        "step_bias": jnp.clip(jax.random.uniform(keys[4], (HEADS,), jnp.float32, -1.0, 1.0) * level_of(keys[4], (HEADS,), ((0, 4),), -0.4, 0.0), -1.0, 1.0),
        "decay_log": jnp.clip(-5.8 + 3.0000002 * jax.random.uniform(keys[5], (HEADS,), jnp.float32) ** level_of(keys[5], (HEADS,), ((0, 4),), -0.2, 0.2), -5.8, -2.8),
        "skip_gain": jnp.clip(0.5 + 1.0 * jax.random.uniform(keys[6], (HEADS,), jnp.float32) ** level_of(keys[6], (HEADS,), ((0, 4),), -0.2, 0.2), 0.5, 1.5),
        "norm_gain": jnp.clip(1.0 + 0.18 * jax.random.normal(keys[7], (HEADS * HEAD_SIZE,), jnp.float32), 0.1, 1.9),
        "cache_states": gaussian(part_splits[8], (SLOTS, HEADS, HEAD_SIZE, STATE_SIZE), 1.0, 6.0, ((1, 4), (2, 4))),
        "slot_decay": jnp.clip(0.2 + 0.7 * jax.random.uniform(part_splits[9], (SLOTS, HEADS), jnp.float32) ** level_of(part_splits[9], (SLOTS, HEADS), ((1, 4),), -0.2, 0.2), 0.2, 0.9),
        "template_state": gaussian(part_splits[10], (HEADS, HEAD_SIZE, STATE_SIZE), 1.0, 6.0, ((0, 4), (1, 4))),
        "slot_ids": touch_ends(jax.random.randint(part_splits[11], (ROWS,), 0, SLOTS), jax.random.fold_in(part_splits[11], 1), 0, SLOTS - 1).astype(jnp.int32),
        "row_lengths": touch_ends(jax.random.randint(part_splits[12], (ROWS,), TOKENS_ROW // 2, TOKENS_ROW + 1), jax.random.fold_in(part_splits[12], 1), TOKENS_ROW // 2, TOKENS_ROW).astype(jnp.int32),
        "row_offsets": touch_ends(jax.random.randint(part_splits[13], (ROWS,), 0, TOKENS_ROW // 4), jax.random.fold_in(part_splits[13], 1), 0, (TOKENS_ROW // 4) - 1).astype(jnp.int32),
    }


def reference(ssm_input, input_proj, output_proj, step_raw, step_bias, decay_log, skip_gain, norm_gain, cache_states, slot_decay, template_state, slot_ids, row_lengths, row_offsets):
    position = jnp.arange(TOKENS_ROW, dtype=jnp.int32)
    causal = position[:, None] >= position[None, :]
    head_group = jnp.arange(HEADS, dtype=jnp.int32) // GROUP_HEADS

    def one_row(items):
        values, inputs, readout, raw, slot, length, offset = items
        alive = position < length
        step_size = jnp.where(alive[None, :], jax.nn.softplus(raw + step_bias[:, None]), 0.0)
        logdecay = jnp.cumsum(-jnp.exp(decay_log)[:, None] * step_size, axis=1)
        resumed = (cache_states[slot].astype(jnp.float32) + slot_decay[slot][:, None, None] * template_state.astype(jnp.float32)).astype(jnp.bfloat16)
        inputs_g = inputs.reshape(TOKENS_ROW, GROUPS, STATE_SIZE)
        readout_g = readout.reshape(TOKENS_ROW, GROUPS, STATE_SIZE)
        gram = jnp.einsum('sgn,ugn->gsu', readout_g.astype(jnp.float32), inputs_g.astype(jnp.float32))
        gram_heads = gram[head_group]
        spread = jnp.where(causal[None], logdecay[:, :, None] - logdecay[:, None, :], 0.0)
        weights = jnp.where(causal[None], gram_heads * jnp.exp(spread) * step_size[:, None, :], 0.0).astype(jnp.bfloat16)
        heads_x = values.reshape(TOKENS_ROW, HEADS, HEAD_SIZE)
        intra = jnp.einsum('hsu,uhp->shp', weights.astype(jnp.float32), heads_x.astype(jnp.float32))
        readout_h = readout_g[:, head_group, :]
        carried = jnp.einsum('shn,hpn->shp', readout_h.astype(jnp.float32), resumed.astype(jnp.float32)) * jnp.exp(logdecay).T[:, :, None]
        scan = intra + carried + skip_gain[None, :, None] * heads_x.astype(jnp.float32)
        grouped = scan.reshape(TOKENS_ROW, GROUPS, GROUP_HEADS * HEAD_SIZE)
        meansq = lax.optimization_barrier(jnp.mean(grouped * grouped, axis=-1, keepdims=True))
        normed = (grouped * lax.rsqrt(meansq + 1e-05)).reshape(TOKENS_ROW, HEADS * HEAD_SIZE) * norm_gain
        keep = alive & (position >= offset)
        mixed = jnp.where(keep[:, None], normed, 0.0).astype(jnp.bfloat16)
        tail = jnp.exp(logdecay[:, -1:] - logdecay) * step_size
        carry = (tail.T[:, :, None] * heads_x.astype(jnp.float32)).astype(jnp.bfloat16)
        inputs_h = inputs_g[:, head_group, :]
        state = jnp.einsum('uhp,uhn->hpn', carry.astype(jnp.float32), inputs_h.astype(jnp.float32))
        state = state + jnp.exp(logdecay[:, -1])[:, None, None] * resumed.astype(jnp.float32)
        return (mixed, state.astype(jnp.bfloat16))
    mixed, new_states = lax.map(one_row, (ssm_input, input_proj, output_proj, step_raw, slot_ids, row_lengths, row_offsets))
    return (mixed, new_states)
```

```python
import functools

import jax
import jax.numpy as jnp
from jax import lax
from jax.experimental import pallas as pl
from jax.experimental.pallas import tpu as pltpu
from jax.sharding import PartitionSpec as P

HEAD_SIZE = 64
GROUP_HEADS = 32
CHUNK = 128
LANES = 256
F32 = jnp.float32
BF16 = jnp.bfloat16
VMEM = pl.BlockSpec(memory_space=pltpu.VMEM)
SMEM = pl.BlockSpec(memory_space=pltpu.SMEM)


def split3(v):
    hi = v.astype(BF16).astype(F32)
    mid = (v - hi).astype(BF16).astype(F32)
    return hi, mid, v - hi - mid


def column(row, heads):
    eye = lax.broadcasted_iota(jnp.int32, (heads, heads), 0) == lax.broadcasted_iota(
        jnp.int32, (heads, heads), 1
    )
    return jnp.sum(jnp.where(eye, row, 0.0), axis=1, keepdims=True)


def spread_matrix(heads, lanes):
    term = lax.broadcasted_iota(jnp.int32, (128, lanes), 0)
    lane = lax.broadcasted_iota(jnp.int32, (128, lanes), 1)
    hit = ((term % heads) == (lane // HEAD_SIZE)) & (term < 3 * heads)
    return jnp.where(hit, 1.0, 0.0).astype(BF16)


def stacked(v):
    heads, length = v.shape
    hi, mid, lo = split3(v)
    full = jnp.concatenate([hi, mid, lo, jnp.zeros((128 - 3 * heads, length), F32)], axis=0)
    return full.T.astype(BF16)


def scan_steps(raw_ref, bias_ref, decay_ref, alive_count):
    heads, length = raw_ref.shape
    bias = column(bias_ref[...], heads)
    rate = -jnp.exp(column(decay_ref[...], heads))
    position = lax.broadcasted_iota(jnp.int32, (heads, length), 1)
    raw = raw_ref[...] + bias
    soft = jnp.maximum(raw, 0.0) + jnp.log1p(jnp.exp(-jnp.abs(raw)))
    step = jnp.where(position < alive_count, soft, 0.0)
    drop = rate * step
    upper = (
        lax.broadcasted_iota(jnp.int32, (CHUNK, CHUNK), 0)
        <= lax.broadcasted_iota(jnp.int32, (CHUNK, CHUNK), 1)
    )
    upper = jnp.where(upper, 1.0, 0.0).astype(BF16)
    base = jnp.zeros((heads, 1), F32)
    parts, starts = [], []
    for c in range(length // CHUNK):
        terms = jnp.concatenate(split3(drop[:, c * CHUNK : (c + 1) * CHUNK]), axis=0)
        sums = jnp.dot(terms.astype(BF16), upper, preferred_element_type=F32)
        run = sums[:heads] + sums[heads : 2 * heads] + sums[2 * heads :]
        starts.append(base)
        parts.append(run + base)
        base = base + run[:, CHUNK - 1 :]
    return step, parts, starts, base


def state_kernel(
    slot_ref, length_ref, raw_ref, bias_ref, decay_ref, x_ref, b_ref, *refs, ways, dp_name
):
    pieces, meta_ref, spread_ref, tail_ref, bt_ref, hold = (
        refs[:ways],
        refs[ways],
        refs[ways + 1],
        refs[ways + 2],
        refs[ways + 3],
        refs[ways + 4],
    )
    heads, length = raw_ref.shape
    width = heads * HEAD_SIZE
    chan = HEAD_SIZE // ways
    step, parts, _, end = scan_steps(raw_ref, bias_ref, decay_ref, length_ref[0])
    logdecay = jnp.concatenate(parts, axis=1)
    tail_ref[...] = stacked(jnp.exp(end - logdecay) * step)
    bt_ref[...] = b_ref[...].T
    spread_ref[...] = spread_matrix(heads, width)
    lane = lax.broadcasted_iota(jnp.int32, (8, 128), 1)
    eye = lax.broadcasted_iota(jnp.int32, (heads, 128), 0) == lax.broadcasted_iota(
        jnp.int32, (heads, 128), 1
    )
    last = jnp.sum(jnp.where(eye, jnp.exp(end), 0.0), axis=0, keepdims=True)
    slot = slot_ref[0].astype(F32)
    meta_ref[...] = jnp.where(lane == heads, slot, jnp.broadcast_to(last, (8, 128)))

    per = LANES // HEAD_SIZE

    def tile(t, carry):
        at = pl.ds(pl.multiple_of(t * LANES, LANES), LANES)
        scale = jnp.dot(tail_ref[...], spread_ref[:, at], preferred_element_type=F32)
        moved = (scale * x_ref[:, at].astype(F32)).astype(BF16)
        state = jnp.dot(bt_ref[...], moved, preferred_element_type=F32)
        turned = state.T.astype(BF16).reshape(per, ways, chan, 128)
        rows = pl.ds(pl.multiple_of(t * per * chan, per * chan), per * chan)
        for d in range(ways):
            hold[d, rows, :] = turned[:, d].reshape(per * chan, 128)
        return carry

    lax.fori_loop(0, width // LANES, tile, 0)
    if ways == 1:
        pieces[0][...] = hold[0]
    else:
        me = lax.axis_index(dp_name)
        for k in range(ways):
            pieces[k][...] = hold[me ^ k]


def row_spread(row, heads, rows):
    terms = jnp.concatenate(split3(row) + (jnp.zeros((1, 128 - 3 * heads), F32),), axis=1)
    lanes = jnp.broadcast_to(terms, (128, 128)).astype(BF16)
    at = lax.broadcasted_iota(jnp.int32, (rows, 128), 0) // (rows // heads)
    term = lax.broadcasted_iota(jnp.int32, (rows, 128), 1)
    pick = jnp.where((term % heads == at) & (term < 3 * heads), 1.0, 0.0).astype(BF16)
    return lax.dot_general(pick, lanes, (((1,), (1,)), ((), ())), preferred_element_type=F32)


def resume_kernel(*refs, ways, heads):
    metas, cache_ref, decay_ref, template_ref = refs[:ways], *refs[ways : ways + 3]
    outs = refs[ways + 3 :]
    rows = template_ref.shape[0]
    lane = lax.broadcasted_iota(jnp.int32, (8, 128), 1)
    template = template_ref[...].astype(F32)
    for k in range(ways):
        slot = jnp.max(jnp.where(lane == heads, metas[k][...], 0.0)).astype(jnp.int32)
        factor = row_spread(decay_ref[pl.ds(slot, 1), :], heads, rows)
        outs[k][...] = (cache_ref[slot].astype(F32) + factor * template).astype(BF16)


def intra_kernel(
    after_ref,
    length_ref,
    raw_ref,
    bias_ref,
    decay_ref,
    skip_ref,
    x_ref,
    b_ref,
    c_ref,
    y_ref,
    grow_ref,
    spread_ref,
    in_ref,
    out_ref,
    whole_ref,
    mix_ref,
    ends_ref,
):
    heads, length = raw_ref.shape
    width = heads * HEAD_SIZE
    chunks = length // CHUNK
    step, parts, starts, end = scan_steps(raw_ref, bias_ref, decay_ref, length_ref[0])
    spread_ref[...] = spread_matrix(heads, width)
    causal = lax.broadcasted_iota(jnp.int32, (CHUNK, CHUNK), 0) >= lax.broadcasted_iota(
        jnp.int32, (CHUNK, CHUNK), 1
    )
    ends = []
    for c in range(chunks):
        at = slice(c * CHUNK, (c + 1) * CHUNK)
        inside = parts[c] - starts[c]
        in_ref[at, :] = stacked(jnp.exp(-inside) * step[:, at])
        out_ref[at, :] = stacked(jnp.exp(inside))
        whole_ref[at, :] = stacked(jnp.exp(parts[c]))
        nxt = starts[c + 1] if c + 1 < chunks else end
        ends.append(jnp.exp(nxt - starts[c]))
        gram = lax.dot_general(
            c_ref[at, :], b_ref[at, :], (((1,), (1,)), ((), ())), preferred_element_type=F32
        )
        mix_ref[at, :CHUNK] = jnp.where(causal, gram, 0.0).astype(BF16)
        mix_ref[at, CHUNK:] = c_ref[at, :]
    lane = lax.broadcasted_iota(jnp.int32, (heads, 128), 1)
    pad = jnp.zeros((heads, 128), F32)
    for c in range(chunks):
        pad = jnp.where(lane == c, ends[c], pad)
    ends_ref[...] = stacked(pad)
    skip_row = jnp.concatenate(split3(skip_ref[...]) + (jnp.zeros((1, 128 - 3 * heads), F32),), axis=1)
    skip_rows = jnp.broadcast_to(skip_row, (8, 128)).astype(BF16)

    def tile(t, carry):
        at = pl.ds(pl.multiple_of(t * LANES, LANES), LANES)
        hot = spread_ref[:, at]
        skip = jnp.dot(skip_rows, hot, preferred_element_type=F32)[0:1]
        decay = jnp.dot(ends_ref[0:8, :], hot, preferred_element_type=F32)
        state = jnp.zeros((128, LANES), F32)
        for c in range(chunks):
            rows = slice(c * CHUNK, (c + 1) * CHUNK)
            x = x_ref[rows, at].astype(F32)
            inner = jnp.dot(in_ref[rows, :], hot, preferred_element_type=F32)
            moved = (x * inner).astype(BF16)
            both = jnp.concatenate([moved, state.astype(BF16)], axis=0)
            mixed = jnp.dot(mix_ref[rows, :], both, preferred_element_type=F32)
            outer = jnp.dot(out_ref[rows, :], hot, preferred_element_type=F32)
            y_ref[rows, at] = outer * mixed + skip * x
            grow_ref[rows, at] = jnp.dot(whole_ref[rows, :], hot, preferred_element_type=F32)
            if c + 1 < chunks:
                fresh = lax.dot_general(
                    b_ref[rows, :], moved, (((0,), (0,)), ((), ())), preferred_element_type=F32
                )
                state = decay[c : c + 1] * (state + fresh)
        return carry

    lax.fori_loop(0, width // LANES, tile, 0)


def norm_kernel(length_ref, offset_ref, *refs, ways, dp_name, heads, block):
    pieces = refs[:ways]
    y_ref, grow_ref, c_ref, gain_ref, mixed_ref, hold = refs[ways:]
    chan = HEAD_SIZE // ways
    i = pl.program_id(0)

    @pl.when(i == 0)
    def _():
        if ways == 1:
            hold[...] = pieces[0][...]
        else:
            me = lax.axis_index(dp_name)
            for k in range(ways):
                start = pl.multiple_of((me ^ k) * chan, chan)
                for h in range(heads):
                    hold[pl.ds(h * HEAD_SIZE + start, chan), :] = pieces[k][
                        h * chan : (h + 1) * chan, :
                    ]

    rows = pl.ds(pl.multiple_of(i * block, block), block)
    carried = lax.dot_general(
        c_ref[rows, :], hold[...], (((1,), (1,)), ((), ())), preferred_element_type=F32
    )
    scan = y_ref[rows, :] + grow_ref[rows, :] * carried
    meansq = jnp.mean(scan * scan, axis=1, keepdims=True)
    position = lax.broadcasted_iota(jnp.int32, (block, 1), 0) + i * block
    keep = (position < length_ref[0]) & (position >= offset_ref[0])
    factor = jnp.where(keep, lax.rsqrt(meansq + 1e-05), 0.0)
    mixed_ref[0] = (scan * factor * gain_ref[...]).astype(BF16)


def final_kernel(*refs, ways, dp_name, heads):
    pieces, resumed, metas = refs[:ways], refs[ways : 2 * ways], refs[2 * ways : 3 * ways]
    out_ref = refs[3 * ways]
    rows = pieces[0].shape[0]
    me = lax.axis_index(dp_name)
    for k in range(ways):
        whole = row_spread(metas[k][0:1, :heads], heads, rows)
        out_ref[me ^ k] = (
            pieces[k][...].astype(F32) + whole * resumed[k][...].astype(F32)
        ).astype(BF16)


def cost(flops, size):
    return pl.CostEstimate(flops=flops, bytes_accessed=size, transcendentals=0)


def local(
    ssm_input,
    input_proj,
    output_proj,
    step_raw,
    step_bias,
    decay_log,
    skip_gain,
    norm_gain,
    cache_states,
    slot_decay,
    template_state,
    slot_ids,
    row_lengths,
    row_offsets,
    *,
    dp,
):
    _, length, width = ssm_input.shape
    heads = step_raw.shape[1]
    slots, _, chan, state = cache_states.shape
    direct = dp in (2, 4)
    ways = dp if direct else 1
    rows = heads * HEAD_SIZE // ways
    x, b, c, raw = ssm_input[0], input_proj[0], output_proj[0], step_raw[0]
    bias, decay, skip = step_bias[None], decay_log[None], skip_gain[None]
    piece = jax.ShapeDtypeStruct((rows, state), BF16)
    params = pltpu.CompilerParams(vmem_limit_bytes=24 << 20)

    *local_parts, meta = pl.pallas_call(
        functools.partial(state_kernel, ways=ways, dp_name="dp"),
        out_shape=[piece] * ways + [jax.ShapeDtypeStruct((8, 128), F32)],
        in_specs=[SMEM, SMEM] + [VMEM] * 5,
        out_specs=[VMEM] * (ways + 1),
        scratch_shapes=[
            pltpu.VMEM((128, width), BF16),
            pltpu.VMEM((length, 128), BF16),
            pltpu.VMEM((128, length), BF16),
            pltpu.VMEM((ways, rows, state), BF16),
        ],
        compiler_params=params,
        cost_estimate=cost(2 * length * width * 256, 3 << 20),
        name="state",
    )(slot_ids, row_lengths, raw, bias, decay, x, b)

    def intra(after):
        return pl.pallas_call(
            intra_kernel,
            out_shape=[jax.ShapeDtypeStruct((length, width), F32)] * 2,
            in_specs=[VMEM, SMEM] + [VMEM] * 7,
            out_specs=[VMEM] * 2,
            scratch_shapes=[
                pltpu.VMEM((128, width), BF16),
                pltpu.VMEM((length, 128), BF16),
                pltpu.VMEM((length, 128), BF16),
                pltpu.VMEM((length, 128), BF16),
                pltpu.VMEM((length, 2 * CHUNK), BF16),
                pltpu.VMEM((128, 128), BF16),
            ],
            compiler_params=params,
            cost_estimate=cost(2 * length * width * 1024, 16 << 20),
            name="intra",
        )(after, row_lengths, raw, bias, decay, skip, x, b, c)

    if direct:

        def swap(v, k):
            return lax.ppermute(v, "dp", [(i, i ^ k) for i in range(dp)])

        order = [2, 3, 1] if dp == 4 else [1]
        got = {k: swap(local_parts[k], k) for k in order}
        metas = {0: meta, **{k: swap(meta, k) for k in order}}
        metas = [metas[k] for k in range(dp)]
        resumed = pl.pallas_call(
            functools.partial(resume_kernel, ways=dp, heads=heads),
            out_shape=[piece] * dp,
            in_specs=[VMEM] * (dp + 3),
            out_specs=[VMEM] * dp,
            compiler_params=params,
            cost_estimate=cost(2 * rows * 128 * 128 * dp, 2 << 20),
            name="resume",
        )(
            *metas,
            cache_states.reshape(slots, rows, state),
            slot_decay,
            template_state.reshape(rows, state),
        )
        sent = {k: swap(resumed[k], k) for k in order}
        y, grow = intra(resumed[0][:8, :])
        final = pl.pallas_call(
            functools.partial(final_kernel, ways=dp, dp_name="dp", heads=heads),
            out_shape=jax.ShapeDtypeStruct((dp, rows, state), BF16),
            in_specs=[VMEM] * (3 * dp),
            out_specs=VMEM,
            compiler_params=params,
            cost_estimate=cost(2 * rows * 128 * 128 * dp, 2 << 20),
            name="final",
        )(local_parts[0], *[got[k] for k in range(1, dp)], *resumed, *metas)
        new_states = final.reshape(dp, heads, chan, state)
        arrived = [resumed[0]] + [sent[k] for k in range(1, dp)]
    else:
        metas = lax.all_gather(meta[0], "dp", axis=0)
        ids = metas[:, heads].astype(jnp.int32)
        resumed = (
            cache_states[ids].astype(F32)
            + slot_decay[ids][:, :, None, None] * template_state.astype(F32)[None]
        ).astype(BF16)
        mine = lax.all_to_all(resumed, "dp", split_axis=0, concat_axis=2, tiled=True)
        arrived = [mine.reshape(rows, state)]
        given = lax.all_to_all(
            local_parts[0].reshape(1, heads, HEAD_SIZE, state),
            "dp",
            split_axis=2,
            concat_axis=0,
            tiled=True,
        )
        new_states = (
            given.astype(F32) + metas[:, :heads, None, None] * resumed.astype(F32)
        ).astype(BF16)
        y, grow = intra(local_parts[0][:8, :])

    block = CHUNK
    mixed = pl.pallas_call(
        functools.partial(norm_kernel, ways=ways, dp_name="dp", heads=heads, block=block),
        out_shape=jax.ShapeDtypeStruct((1, length, width), BF16),
        grid=(length // block,),
        in_specs=[SMEM, SMEM] + [VMEM] * (ways + 4),
        out_specs=pl.BlockSpec((1, block, width), lambda i: (0, i, 0)),
        scratch_shapes=[pltpu.VMEM((heads * HEAD_SIZE, state), BF16)],
        compiler_params=params,
        cost_estimate=cost(2 * length * width * 128, 4 << 20),
        name="norm",
    )(row_lengths, row_offsets, *arrived, y, grow, c, norm_gain[None])
    return (mixed, new_states)


def solution(mesh):
    return jax.shard_map(
        functools.partial(local, dp=mesh.shape["dp"]),
        mesh=mesh,
        in_specs=(
            P(("groups", "dp"), None, "tensor"),
            P(("groups", "dp"), None, "tensor"),
            P(("groups", "dp"), None, "tensor"),
            P(("groups", "dp"), "tensor", None),
            P("tensor"),
            P("tensor"),
            P("tensor"),
            P("tensor"),
            P("groups", "tensor", "dp", None),
            P("groups", "tensor"),
            P(("groups", "tensor"), "dp", None),
            P(("groups", "dp")),
            P(("groups", "dp")),
            P(("groups", "dp")),
        ),
        out_specs=(P(("groups", "dp"), None, "tensor"), P("groups", "tensor", "dp", None)),
        check_vma=False,
    )
```

```python
import functools

import jax
import jax.numpy as jnp
from jax import lax
from jax.experimental import pallas as pl
from jax.experimental.pallas import tpu as pltpu
from jax.sharding import PartitionSpec as P

HEAD_SIZE = 64
GROUP_HEADS = 32
CHUNK = 128
LANES = 256
F32 = jnp.float32
BF16 = jnp.bfloat16
VMEM = pl.BlockSpec(memory_space=pltpu.VMEM)
SMEM = pl.BlockSpec(memory_space=pltpu.SMEM)


def split3(v):
    hi = v.astype(BF16).astype(F32)
    mid = (v - hi).astype(BF16).astype(F32)
    return hi, mid, v - hi - mid


def column(row, heads):
    eye = lax.broadcasted_iota(jnp.int32, (heads, heads), 0) == lax.broadcasted_iota(
        jnp.int32, (heads, heads), 1
    )
    return jnp.sum(jnp.where(eye, row, 0.0), axis=1, keepdims=True)


def spread_matrix(heads, lanes):
    term = lax.broadcasted_iota(jnp.int32, (128, 1), 0)
    head = term
    for k in (1, 2):
        head = jnp.where(term >= k * heads, term - k * heads, head)
    head = jnp.where(term >= 3 * heads, -1, head)
    first = head * HEAD_SIZE
    lane = lax.broadcasted_iota(jnp.int32, (1, lanes), 1)
    hit = jnp.where(lane >= first, 1.0, 0.0) - jnp.where(lane >= first + HEAD_SIZE, 1.0, 0.0)
    return jnp.where(head >= 0, hit, 0.0).astype(BF16)


def stacked(v):
    heads, length = v.shape
    hi, mid, lo = split3(v)
    full = jnp.concatenate([hi, mid, lo, jnp.zeros((128 - 3 * heads, length), F32)], axis=0)
    return full.T.astype(BF16)


def scan_steps(raw, bias_row, decay_row, alive_count):
    heads, length = raw.shape
    bias = column(bias_row, heads)
    rate = -jnp.exp(column(decay_row, heads))
    position = lax.broadcasted_iota(jnp.int32, (heads, length), 1)
    raw = raw + bias
    soft = jnp.maximum(raw, 0.0) + jnp.log1p(jnp.exp(-jnp.abs(raw)))
    step = jnp.where(position < alive_count, soft, 0.0)
    drop = rate * step
    upper = (
        lax.broadcasted_iota(jnp.int32, (CHUNK, CHUNK), 0)
        <= lax.broadcasted_iota(jnp.int32, (CHUNK, CHUNK), 1)
    )
    upper = jnp.where(upper, 1.0, 0.0).astype(BF16)
    chunks = length // CHUNK
    terms = [t for c in range(chunks) for t in split3(drop[:, c * CHUNK : (c + 1) * CHUNK])]
    sums = jnp.dot(
        jnp.concatenate(terms, axis=0).astype(BF16), upper, preferred_element_type=F32
    )
    base = jnp.zeros((heads, 1), F32)
    parts = []
    for c in range(chunks):
        i = 3 * c * heads
        run = sums[i : i + heads] + sums[i + heads : i + 2 * heads] + sums[i + 2 * heads : i + 3 * heads]
        parts.append(run + base)
        base = base + run[:, CHUNK - 1 :]
    return step, jnp.concatenate(parts, axis=1)


def state_kernel(*refs, ways, dp_name, loads):
    sources, refs = refs[:loads], refs[loads:]
    pieces, refs = refs[:ways], refs[ways:]
    meta_ref, spread_ref, step_ref, log_ref, *refs = refs
    held, (tail_ref, hold, sems) = refs[:loads], refs[loads:]
    raw_ref, bias_ref, decay_ref, length_ref, slot_ref, b_ref, x_ref = held[:7]
    heads, length = raw_ref.shape
    width = heads * HEAD_SIZE
    chan = HEAD_SIZE // ways
    copies = [
        pltpu.make_async_copy(source, target, sems.at[i])
        for i, (source, target) in enumerate(zip(sources, held))
    ]
    for copy in copies:
        copy.start()
    spread_ref[...] = spread_matrix(heads, width)
    for copy in copies[:4]:
        copy.wait()
    step, logdecay = scan_steps(raw_ref[...], bias_ref[...], decay_ref[...], length_ref[...])
    step_ref[...] = step
    log_ref[...] = logdecay
    end = logdecay[:, length - 1 :]
    tail_ref[...] = stacked(jnp.exp(end - logdecay) * step)
    lane = lax.broadcasted_iota(jnp.int32, (8, 128), 1)
    eye = lax.broadcasted_iota(jnp.int32, (heads, 128), 0) == lax.broadcasted_iota(
        jnp.int32, (heads, 128), 1
    )
    last = jnp.sum(jnp.where(eye, jnp.exp(end), 0.0), axis=0, keepdims=True)
    for copy in copies[4:7]:
        copy.wait()
    slot = slot_ref[...].astype(F32)
    meta_ref[...] = jnp.where(lane == heads, slot, jnp.broadcast_to(last, (8, 128)))
    turned_b = b_ref[...].T
    per = LANES // HEAD_SIZE
    for t in range(width // LANES):
        at = slice(t * LANES, (t + 1) * LANES)
        scale = jnp.dot(tail_ref[...], spread_ref[:, at], preferred_element_type=F32)
        moved = (scale * x_ref[:, at].astype(F32)).astype(BF16)
        state = jnp.dot(turned_b, moved, preferred_element_type=F32)
        turned = state.T.astype(BF16).reshape(per, ways, chan, 128)
        for d in range(ways):
            hold[d, t * per * chan : (t + 1) * per * chan, :] = turned[:, d].reshape(per * chan, 128)
    if ways == 1:
        pieces[0][...] = hold[0]
    else:
        me = lax.axis_index(dp_name)
        for k in range(ways):
            pieces[k][...] = hold[me ^ k]
    for copy in copies[7:]:
        copy.wait()


def row_spread(row, heads, rows):
    terms = jnp.concatenate(split3(row) + (jnp.zeros((1, 128 - 3 * heads), F32),), axis=1)
    lanes = jnp.broadcast_to(terms, (128, 128)).astype(BF16)
    at = lax.broadcasted_iota(jnp.int32, (rows, 128), 0) // (rows // heads)
    term = lax.broadcasted_iota(jnp.int32, (rows, 128), 1)
    pick = jnp.where((term % heads == at) & (term < 3 * heads), 1.0, 0.0).astype(BF16)
    return lax.dot_general(pick, lanes, (((1,), (1,)), ((), ())), preferred_element_type=F32)


def resume_kernel(*refs, ways, heads):
    metas, cache_ref, decay_ref, template_ref = refs[:ways], *refs[ways : ways + 3]
    outs = refs[ways + 3 :]
    rows = template_ref.shape[0]
    lane = lax.broadcasted_iota(jnp.int32, (8, 128), 1)
    template = template_ref[...].astype(F32)
    for k in range(ways):
        slot = jnp.max(jnp.where(lane == heads, metas[k][...], 0.0)).astype(jnp.int32)
        factor = row_spread(decay_ref[pl.ds(slot, 1), :], heads, rows)
        outs[k][...] = (cache_ref[slot].astype(F32) + factor * template).astype(BF16)


def intra_kernel(
    after_ref,
    step_ref,
    log_ref,
    skip_ref,
    spread_ref,
    x_ref,
    b_ref,
    c_ref,
    y_ref,
    grow_ref,
    in_ref,
    out_ref,
    whole_ref,
    mix_ref,
    ends_ref,
):
    heads, length = step_ref.shape
    width = heads * HEAD_SIZE
    chunks = length // CHUNK
    causal = lax.broadcasted_iota(jnp.int32, (CHUNK, CHUNK), 0) >= lax.broadcasted_iota(
        jnp.int32, (CHUNK, CHUNK), 1
    )
    lane = lax.broadcasted_iota(jnp.int32, (heads, 128), 1)
    ends = jnp.zeros((heads, 128), F32)
    start = jnp.zeros((heads, 1), F32)
    for c in range(chunks):
        at = slice(c * CHUNK, (c + 1) * CHUNK)
        logdecay = log_ref[:, at]
        inside = logdecay - start
        in_ref[at, :] = stacked(jnp.exp(-inside) * step_ref[:, at])
        out_ref[at, :] = stacked(jnp.exp(inside))
        whole_ref[at, :] = stacked(jnp.exp(logdecay))
        ends = jnp.where(lane == c, jnp.exp(inside[:, CHUNK - 1 :]), ends)
        start = logdecay[:, CHUNK - 1 :]
        gram = lax.dot_general(
            c_ref[at, :], b_ref[at, :], (((1,), (1,)), ((), ())), preferred_element_type=F32
        )
        mix_ref[at, :CHUNK] = jnp.where(causal, gram, 0.0).astype(BF16)
        mix_ref[at, CHUNK:] = c_ref[at, :]
    ends_ref[...] = stacked(ends)
    skip_row = jnp.concatenate(split3(skip_ref[...]) + (jnp.zeros((1, 128 - 3 * heads), F32),), axis=1)
    skip_rows = jnp.broadcast_to(skip_row, (8, 128)).astype(BF16)

    for t in range(width // LANES):
        at = slice(t * LANES, (t + 1) * LANES)
        hot = spread_ref[:, at]
        skip = jnp.dot(skip_rows, hot, preferred_element_type=F32)[0:1]
        decay = jnp.dot(ends_ref[0:8, :], hot, preferred_element_type=F32)
        state = jnp.zeros((128, LANES), F32)
        for c in range(chunks):
            rows = slice(c * CHUNK, (c + 1) * CHUNK)
            x = x_ref[rows, at].astype(F32)
            inner = jnp.dot(in_ref[rows, :], hot, preferred_element_type=F32)
            moved = (x * inner).astype(BF16)
            both = jnp.concatenate([moved, state.astype(BF16)], axis=0)
            mixed = jnp.dot(mix_ref[rows, :], both, preferred_element_type=F32)
            outer = jnp.dot(out_ref[rows, :], hot, preferred_element_type=F32)
            y_ref[rows, at] = outer * mixed + skip * x
            grow_ref[rows, at] = jnp.dot(whole_ref[rows, :], hot, preferred_element_type=F32)
            if c + 1 < chunks:
                fresh = lax.dot_general(
                    b_ref[rows, :], moved, (((0,), (0,)), ((), ())), preferred_element_type=F32
                )
                state = decay[c : c + 1] * (state + fresh)


def norm_kernel(*refs, ways, dp_name, heads, block):
    pieces, refs = refs[:ways], refs[ways:]
    length_ref, offset_ref, y_ref, grow_ref, c_ref, gain_ref, mixed_ref, hold, done, sems = refs
    chan = HEAD_SIZE // ways
    if ways == 1:
        hold[...] = pieces[0][...]
    else:
        me = lax.axis_index(dp_name)
        for k in range(ways):
            start = pl.multiple_of((me ^ k) * chan, chan)
            for h in range(heads):
                hold[pl.ds(h * HEAD_SIZE + start, chan), :] = pieces[k][h * chan : (h + 1) * chan, :]
    position = lax.broadcasted_iota(jnp.int32, (block, 1), 0)
    copies = []
    for i in range(y_ref.shape[0] // block):
        rows = slice(i * block, (i + 1) * block)
        carried = lax.dot_general(
            c_ref[rows, :], hold[...], (((1,), (1,)), ((), ())), preferred_element_type=F32
        )
        scan = y_ref[rows, :] + grow_ref[rows, :] * carried
        meansq = jnp.mean(scan * scan, axis=1, keepdims=True)
        keep = (position + i * block < length_ref[...]) & (position + i * block >= offset_ref[...])
        factor = jnp.where(keep, lax.rsqrt(meansq + 1e-05), 0.0)
        done[rows, :] = (scan * factor * gain_ref[...]).astype(BF16)
        copy = pltpu.make_async_copy(done.at[rows, :], mixed_ref.at[0, rows, :], sems.at[i])
        copy.start()
        copies.append(copy)
    for copy in copies:
        copy.wait()


def final_kernel(*refs, ways, dp_name, heads):
    pieces, resumed, metas = refs[:ways], refs[ways : 2 * ways], refs[2 * ways : 3 * ways]
    out_ref = refs[3 * ways]
    rows = pieces[0].shape[0]
    me = lax.axis_index(dp_name)
    for k in range(ways):
        whole = row_spread(metas[k][0:1, :heads], heads, rows)
        out_ref[me ^ k] = (
            pieces[k][...].astype(F32) + whole * resumed[k][...].astype(F32)
        ).astype(BF16)


def cost(flops, size):
    return pl.CostEstimate(flops=flops, bytes_accessed=size, transcendentals=0)


def local(
    ssm_input,
    input_proj,
    output_proj,
    step_raw,
    step_bias,
    decay_log,
    skip_gain,
    norm_gain,
    cache_states,
    slot_decay,
    template_state,
    slot_ids,
    row_lengths,
    row_offsets,
    *,
    dp,
):
    _, length, width = ssm_input.shape
    heads = step_raw.shape[1]
    slots, _, chan, state = cache_states.shape
    direct = dp in (2, 4)
    ways = dp if direct else 1
    rows = heads * HEAD_SIZE // ways
    piece = jax.ShapeDtypeStruct((rows, state), BF16)
    params = pltpu.CompilerParams(vmem_limit_bytes=24 << 20)
    loaded = [
        step_raw[0],
        step_bias[None],
        decay_log[None],
        row_lengths[None],
        slot_ids[None],
        input_proj[0],
        ssm_input[0],
        output_proj[0],
        skip_gain[None],
        norm_gain[None],
        row_offsets[None],
        template_state.reshape(-1, state),
        slot_decay,
    ]
    shape_of = lambda v: jax.ShapeDtypeStruct(v.shape, v.dtype)
    outs = pl.pallas_call(
        functools.partial(state_kernel, ways=ways, dp_name="dp", loads=len(loaded)),
        out_shape=[piece] * ways
        + [
            jax.ShapeDtypeStruct((8, 128), F32),
            jax.ShapeDtypeStruct((128, width), BF16),
            jax.ShapeDtypeStruct((heads, length), F32),
            jax.ShapeDtypeStruct((heads, length), F32),
        ]
        + [shape_of(v) for v in loaded],
        in_specs=[pl.BlockSpec(memory_space=pltpu.HBM)] * len(loaded),
        out_specs=[VMEM] * (ways + 4 + len(loaded)),
        scratch_shapes=[
            pltpu.VMEM((length, 128), BF16),
            pltpu.VMEM((ways, rows, state), BF16),
            pltpu.SemaphoreType.DMA((len(loaded),)),
        ],
        compiler_params=params,
        cost_estimate=cost(2 * length * width * 256, 3 << 20),
        name="state",
    )(*loaded)
    local_parts, (meta, spread, step, logdecay, *held) = outs[:ways], outs[ways:]
    _, _, _, alive, _, b, x, c, skip, gain, offset, template, decays = held

    def intra(after):
        return pl.pallas_call(
            intra_kernel,
            out_shape=[jax.ShapeDtypeStruct((length, width), F32)] * 2,
            in_specs=[VMEM] * 8,
            out_specs=[VMEM] * 2,
            scratch_shapes=[
                pltpu.VMEM((length, 128), BF16),
                pltpu.VMEM((length, 128), BF16),
                pltpu.VMEM((length, 128), BF16),
                pltpu.VMEM((length, 2 * CHUNK), BF16),
                pltpu.VMEM((128, 128), BF16),
            ],
            compiler_params=params,
            cost_estimate=cost(2 * length * width * 1024, 16 << 20),
            name="intra",
        )(after, step, logdecay, skip, spread, x, b, c)

    if direct:

        def swap(v, k):
            return lax.ppermute(v, "dp", [(i, i ^ k) for i in range(dp)])

        order = [2, 3, 1] if dp == 4 else [1]
        got = {k: swap(local_parts[k], k) for k in order}
        metas = {0: meta, **{k: swap(meta, k) for k in order}}
        metas = [metas[k] for k in range(dp)]
        resumed = pl.pallas_call(
            functools.partial(resume_kernel, ways=dp, heads=heads),
            out_shape=[piece] * dp,
            in_specs=[VMEM] * (dp + 3),
            out_specs=[VMEM] * dp,
            compiler_params=params,
            cost_estimate=cost(2 * rows * 128 * 128 * dp, 2 << 20),
            name="resume",
        )(
            *metas,
            cache_states.reshape(slots, rows, state),
            decays,
            template,
        )
        sent = {k: swap(resumed[k], k) for k in order}
        y, grow = intra(resumed[0][:8, :])
        final = pl.pallas_call(
            functools.partial(final_kernel, ways=dp, dp_name="dp", heads=heads),
            out_shape=jax.ShapeDtypeStruct((dp, rows, state), BF16),
            in_specs=[VMEM] * (3 * dp),
            out_specs=VMEM,
            compiler_params=params,
            cost_estimate=cost(2 * rows * 128 * 128 * dp, 2 << 20),
            name="final",
        )(local_parts[0], *[got[k] for k in range(1, dp)], *resumed, *metas)
        new_states = final.reshape(dp, heads, chan, state)
        arrived = [resumed[0]] + [sent[k] for k in range(1, dp)]
    else:
        metas = lax.all_gather(meta[0], "dp", axis=0)
        ids = metas[:, heads].astype(jnp.int32)
        resumed = (
            cache_states[ids].astype(F32)
            + slot_decay[ids][:, :, None, None] * template_state.astype(F32)[None]
        ).astype(BF16)
        mine = lax.all_to_all(resumed, "dp", split_axis=0, concat_axis=2, tiled=True)
        arrived = [mine.reshape(rows, state)]
        given = lax.all_to_all(
            local_parts[0].reshape(1, heads, HEAD_SIZE, state),
            "dp",
            split_axis=2,
            concat_axis=0,
            tiled=True,
        )
        new_states = (
            given.astype(F32) + metas[:, :heads, None, None] * resumed.astype(F32)
        ).astype(BF16)
        y, grow = intra(local_parts[0][:8, :])

    block = CHUNK
    mixed = pl.pallas_call(
        functools.partial(norm_kernel, ways=ways, dp_name="dp", heads=heads, block=block),
        out_shape=jax.ShapeDtypeStruct((1, length, width), BF16),
        in_specs=[VMEM] * (ways + 6),
        out_specs=pl.BlockSpec(memory_space=pltpu.HBM),
        scratch_shapes=[
            pltpu.VMEM((heads * HEAD_SIZE, state), BF16),
            pltpu.VMEM((length, width), BF16),
            pltpu.SemaphoreType.DMA((length // block,)),
        ],
        compiler_params=params,
        cost_estimate=cost(2 * length * width * 128, 4 << 20),
        name="norm",
    )(*arrived, alive, offset, y, grow, c, gain)
    return (mixed, new_states)


def solution(mesh):
    return jax.shard_map(
        functools.partial(local, dp=mesh.shape["dp"]),
        mesh=mesh,
        in_specs=(
            P(("groups", "dp"), None, "tensor"),
            P(("groups", "dp"), None, "tensor"),
            P(("groups", "dp"), None, "tensor"),
            P(("groups", "dp"), "tensor", None),
            P("tensor"),
            P("tensor"),
            P("tensor"),
            P("tensor"),
            P("groups", "tensor", "dp", None),
            P("groups", "tensor"),
            P(("groups", "tensor"), "dp", None),
            P(("groups", "dp")),
            P(("groups", "dp")),
            P(("groups", "dp")),
        ),
        out_specs=(P(("groups", "dp"), None, "tensor"), P("groups", "tensor", "dp", None)),
        check_vma=False,
    )
```

```python
import functools

import jax
import jax.numpy as jnp
from jax import lax
from jax.experimental import pallas as pl
from jax.experimental.pallas import tpu as pltpu
from jax.sharding import PartitionSpec as P

HEAD_SIZE = 64
GROUP_HEADS = 32
CHUNK = 128
LANES = 256
F32 = jnp.float32
BF16 = jnp.bfloat16
VMEM = pl.BlockSpec(memory_space=pltpu.VMEM)
SMEM = pl.BlockSpec(memory_space=pltpu.SMEM)


def split3(v):
    hi = v.astype(BF16).astype(F32)
    mid = (v - hi).astype(BF16).astype(F32)
    return hi, mid, v - hi - mid


def column(row, heads):
    eye = lax.broadcasted_iota(jnp.int32, (heads, heads), 0) == lax.broadcasted_iota(
        jnp.int32, (heads, heads), 1
    )
    return jnp.sum(jnp.where(eye, row, 0.0), axis=1, keepdims=True)


def spread_matrix(heads, lanes):
    term = lax.broadcasted_iota(jnp.int32, (128, 1), 0)
    head = term
    for k in (1, 2):
        head = jnp.where(term >= k * heads, term - k * heads, head)
    head = jnp.where(term >= 3 * heads, -1, head)
    first = head * HEAD_SIZE
    lane = lax.broadcasted_iota(jnp.int32, (1, lanes), 1)
    hit = jnp.where(lane >= first, 1.0, 0.0) - jnp.where(lane >= first + HEAD_SIZE, 1.0, 0.0)
    return jnp.where(head >= 0, hit, 0.0).astype(BF16)


def stacked(v):
    heads, length = v.shape
    hi, mid, lo = split3(v)
    full = jnp.concatenate([hi, mid, lo, jnp.zeros((128 - 3 * heads, length), F32)], axis=0)
    return full.T.astype(BF16)


def scan_steps(raw, bias_row, decay_row, alive_count):
    heads, length = raw.shape
    bias = column(bias_row, heads)
    rate = -jnp.exp(column(decay_row, heads))
    position = lax.broadcasted_iota(jnp.int32, (heads, length), 1)
    raw = raw + bias
    soft = jnp.maximum(raw, 0.0) + jnp.log1p(jnp.exp(-jnp.abs(raw)))
    step = jnp.where(position < alive_count, soft, 0.0)
    drop = rate * step
    upper = (
        lax.broadcasted_iota(jnp.int32, (CHUNK, CHUNK), 0)
        <= lax.broadcasted_iota(jnp.int32, (CHUNK, CHUNK), 1)
    )
    upper = jnp.where(upper, 1.0, 0.0).astype(BF16)
    chunks = length // CHUNK
    terms = [t for c in range(chunks) for t in split3(drop[:, c * CHUNK : (c + 1) * CHUNK])]
    sums = jnp.dot(
        jnp.concatenate(terms, axis=0).astype(BF16), upper, preferred_element_type=F32
    )
    base = jnp.zeros((heads, 1), F32)
    parts = []
    for c in range(chunks):
        i = 3 * c * heads
        run = sums[i : i + heads] + sums[i + heads : i + 2 * heads] + sums[i + 2 * heads : i + 3 * heads]
        parts.append(run + base)
        base = base + run[:, CHUNK - 1 :]
    return step, jnp.concatenate(parts, axis=1)


def state_kernel(*refs, ways, dp_name, loads):
    sources, refs = refs[:loads], refs[loads:]
    pieces, refs = refs[:ways], refs[ways:]
    meta_ref, spread_ref, step_ref, log_ref, *refs = refs
    held, (tail_ref, hold, sems) = refs[:loads], refs[loads:]
    raw_ref, bias_ref, decay_ref, length_ref, slot_ref, b_ref, x_ref = held[:7]
    heads, length = raw_ref.shape
    width = heads * HEAD_SIZE
    chan = HEAD_SIZE // ways
    copies = [
        pltpu.make_async_copy(source, target, sems.at[i])
        for i, (source, target) in enumerate(zip(sources, held))
    ]
    for copy in copies:
        copy.start()
    spread_ref[...] = spread_matrix(heads, width)
    for copy in copies[:4]:
        copy.wait()
    step, logdecay = scan_steps(raw_ref[...], bias_ref[...], decay_ref[...], length_ref[...])
    step_ref[...] = step
    log_ref[...] = logdecay
    end = logdecay[:, length - 1 :]
    tail_ref[...] = stacked(jnp.exp(end - logdecay) * step)
    lane = lax.broadcasted_iota(jnp.int32, (8, 128), 1)
    eye = lax.broadcasted_iota(jnp.int32, (heads, 128), 0) == lax.broadcasted_iota(
        jnp.int32, (heads, 128), 1
    )
    last = jnp.sum(jnp.where(eye, jnp.exp(end), 0.0), axis=0, keepdims=True)
    for copy in copies[4:7]:
        copy.wait()
    slot = slot_ref[...].astype(F32)
    meta_ref[...] = jnp.where(lane == heads, slot, jnp.broadcast_to(last, (8, 128)))
    turned_b = b_ref[...].T
    per = LANES // HEAD_SIZE
    for t in range(width // LANES):
        at = slice(t * LANES, (t + 1) * LANES)
        scale = jnp.dot(tail_ref[...], spread_ref[:, at], preferred_element_type=F32)
        moved = (scale * x_ref[:, at].astype(F32)).astype(BF16)
        state = jnp.dot(turned_b, moved, preferred_element_type=F32)
        turned = state.T.astype(BF16).reshape(per, ways, chan, 128)
        for d in range(ways):
            hold[d, t * per * chan : (t + 1) * per * chan, :] = turned[:, d].reshape(per * chan, 128)
    if ways == 1:
        pieces[0][...] = hold[0]
    else:
        me = lax.axis_index(dp_name)
        for k in range(ways):
            pieces[k][...] = hold[me ^ k]
    for copy in copies[7:]:
        copy.wait()


def row_spread(row, heads, rows):
    terms = jnp.concatenate(split3(row) + (jnp.zeros((1, 128 - 3 * heads), F32),), axis=1)
    lanes = jnp.broadcast_to(terms, (128, 128)).astype(BF16)
    at = lax.broadcasted_iota(jnp.int32, (rows, 128), 0) // (rows // heads)
    term = lax.broadcasted_iota(jnp.int32, (rows, 128), 1)
    pick = jnp.where((term % heads == at) & (term < 3 * heads), 1.0, 0.0).astype(BF16)
    return lax.dot_general(pick, lanes, (((1,), (1,)), ((), ())), preferred_element_type=F32)


def resume_kernel(*refs, ways, heads):
    metas, cache_ref, decay_ref, template_ref = refs[:ways], *refs[ways : ways + 3]
    outs = refs[ways + 3 :]
    rows = template_ref.shape[0]
    lane = lax.broadcasted_iota(jnp.int32, (8, 128), 1)
    template = template_ref[...].astype(F32)
    for k in range(ways):
        slot = jnp.max(jnp.where(lane == heads, metas[k][...], 0.0)).astype(jnp.int32)
        factor = row_spread(decay_ref[pl.ds(slot, 1), :], heads, rows)
        outs[k][...] = (cache_ref[slot].astype(F32) + factor * template).astype(BF16)


def intra_kernel(
    after_ref,
    step_ref,
    log_ref,
    skip_ref,
    spread_ref,
    x_ref,
    b_ref,
    c_ref,
    y_ref,
    grow_ref,
    in_ref,
    out_ref,
    whole_ref,
    mix_ref,
    ends_ref,
):
    heads, length = step_ref.shape
    width = heads * HEAD_SIZE
    chunks = length // CHUNK
    causal = lax.broadcasted_iota(jnp.int32, (CHUNK, CHUNK), 0) >= lax.broadcasted_iota(
        jnp.int32, (CHUNK, CHUNK), 1
    )
    lane = lax.broadcasted_iota(jnp.int32, (heads, 128), 1)
    ends = jnp.zeros((heads, 128), F32)
    start = jnp.zeros((heads, 1), F32)
    for c in range(chunks):
        at = slice(c * CHUNK, (c + 1) * CHUNK)
        logdecay = log_ref[:, at]
        inside = logdecay - start
        in_ref[at, :] = stacked(jnp.exp(-inside) * step_ref[:, at])
        out_ref[at, :] = stacked(jnp.exp(inside))
        whole_ref[at, :] = stacked(jnp.exp(logdecay))
        ends = jnp.where(lane == c, jnp.exp(inside[:, CHUNK - 1 :]), ends)
        start = logdecay[:, CHUNK - 1 :]
        gram = lax.dot_general(
            c_ref[at, :], b_ref[at, :], (((1,), (1,)), ((), ())), preferred_element_type=F32
        )
        mix_ref[at, :CHUNK] = jnp.where(causal, gram, 0.0).astype(BF16)
        mix_ref[at, CHUNK:] = c_ref[at, :]
    ends_ref[...] = stacked(ends)
    skip_row = jnp.concatenate(split3(skip_ref[...]) + (jnp.zeros((1, 128 - 3 * heads), F32),), axis=1)
    skip_rows = jnp.broadcast_to(skip_row, (8, 128)).astype(BF16)

    for t in range(width // LANES):
        at = slice(t * LANES, (t + 1) * LANES)
        hot = spread_ref[:, at]
        skip = jnp.dot(skip_rows, hot, preferred_element_type=F32)[0:1]
        decay = jnp.dot(ends_ref[0:8, :], hot, preferred_element_type=F32)
        state = jnp.zeros((128, LANES), F32)
        for c in range(chunks):
            rows = slice(c * CHUNK, (c + 1) * CHUNK)
            x = x_ref[rows, at].astype(F32)
            inner = jnp.dot(in_ref[rows, :], hot, preferred_element_type=F32)
            moved = (x * inner).astype(BF16)
            both = jnp.concatenate([moved, state.astype(BF16)], axis=0)
            mixed = jnp.dot(mix_ref[rows, :], both, preferred_element_type=F32)
            outer = jnp.dot(out_ref[rows, :], hot, preferred_element_type=F32)
            y_ref[rows, at] = outer * mixed + skip * x
            grow_ref[rows, at] = jnp.dot(whole_ref[rows, :], hot, preferred_element_type=F32)
            if c + 1 < chunks:
                fresh = lax.dot_general(
                    b_ref[rows, :], moved, (((0,), (0,)), ((), ())), preferred_element_type=F32
                )
                state = decay[c : c + 1] * (state + fresh)


def norm_kernel(*refs, ways, dp_name, heads, block):
    pieces, refs = refs[:ways], refs[ways:]
    length_ref, offset_ref, y_ref, grow_ref, c_ref, gain_ref, mixed_ref, hold, done, sems = refs
    chan = HEAD_SIZE // ways
    if ways == 1:
        hold[...] = pieces[0][...]
    else:
        me = lax.axis_index(dp_name)
        for k in range(ways):
            start = pl.multiple_of((me ^ k) * chan, chan)
            for h in range(heads):
                hold[pl.ds(h * HEAD_SIZE + start, chan), :] = pieces[k][h * chan : (h + 1) * chan, :]
    position = lax.broadcasted_iota(jnp.int32, (block, 1), 0)
    copies = []
    for i in range(y_ref.shape[0] // block):
        rows = slice(i * block, (i + 1) * block)
        carried = lax.dot_general(
            c_ref[rows, :], hold[...], (((1,), (1,)), ((), ())), preferred_element_type=F32
        )
        scan = y_ref[rows, :] + grow_ref[rows, :] * carried
        meansq = jnp.mean(scan * scan, axis=1, keepdims=True)
        keep = (position + i * block < length_ref[...]) & (position + i * block >= offset_ref[...])
        factor = jnp.where(keep, lax.rsqrt(meansq + 1e-05), 0.0)
        done[rows, :] = (scan * factor * gain_ref[...]).astype(BF16)
        copy = pltpu.make_async_copy(done.at[rows, :], mixed_ref.at[0, rows, :], sems.at[i])
        copy.start()
        copies.append(copy)
    for copy in copies:
        copy.wait()


def final_kernel(*refs, ways, dp_name, heads):
    pieces, resumed, metas = refs[:ways], refs[ways : 2 * ways], refs[2 * ways : 3 * ways]
    out_ref = refs[3 * ways]
    rows = pieces[0].shape[0]
    me = lax.axis_index(dp_name)
    for k in range(ways):
        whole = row_spread(metas[k][0:1, :heads], heads, rows)
        out_ref[me ^ k] = (
            pieces[k][...].astype(F32) + whole * resumed[k][...].astype(F32)
        ).astype(BF16)


def pinned(v):
    return v if v.dtype == jnp.int32 else pltpu.with_memory_space_constraint(v, pltpu.HBM)


def cost(flops, size):
    return pl.CostEstimate(flops=flops, bytes_accessed=size, transcendentals=0)


def local(
    ssm_input,
    input_proj,
    output_proj,
    step_raw,
    step_bias,
    decay_log,
    skip_gain,
    norm_gain,
    cache_states,
    slot_decay,
    template_state,
    slot_ids,
    row_lengths,
    row_offsets,
    *,
    dp,
):
    _, length, width = ssm_input.shape
    heads = step_raw.shape[1]
    slots, _, chan, state = cache_states.shape
    direct = dp in (2, 4)
    ways = dp if direct else 1
    rows = heads * HEAD_SIZE // ways
    piece = jax.ShapeDtypeStruct((rows, state), BF16)
    params = pltpu.CompilerParams(vmem_limit_bytes=24 << 20)
    loaded = [
        step_raw[0],
        step_bias[None],
        decay_log[None],
        row_lengths[None],
        slot_ids[None],
        input_proj[0],
        ssm_input[0],
        output_proj[0],
        skip_gain[None],
        norm_gain[None],
        row_offsets[None],
        template_state.reshape(-1, state),
        slot_decay,
    ]
    shape_of = lambda v: jax.ShapeDtypeStruct(v.shape, v.dtype)
    outs = pl.pallas_call(
        functools.partial(state_kernel, ways=ways, dp_name="dp", loads=len(loaded)),
        out_shape=[piece] * ways
        + [
            jax.ShapeDtypeStruct((8, 128), F32),
            jax.ShapeDtypeStruct((128, width), BF16),
            jax.ShapeDtypeStruct((heads, length), F32),
            jax.ShapeDtypeStruct((heads, length), F32),
        ]
        + [shape_of(v) for v in loaded],
        in_specs=[pl.BlockSpec(memory_space=pltpu.HBM)] * len(loaded),
        out_specs=[VMEM] * (ways + 4 + len(loaded)),
        scratch_shapes=[
            pltpu.VMEM((length, 128), BF16),
            pltpu.VMEM((ways, rows, state), BF16),
            pltpu.SemaphoreType.DMA((len(loaded),)),
        ],
        compiler_params=params,
        cost_estimate=cost(2 * length * width * 256, 3 << 20),
        name="state",
    )(*[pinned(v) for v in loaded])
    local_parts, (meta, spread, step, logdecay, *held) = outs[:ways], outs[ways:]
    _, _, _, alive, _, b, x, c, skip, gain, offset, template, decays = held

    def intra(after):
        return pl.pallas_call(
            intra_kernel,
            out_shape=[jax.ShapeDtypeStruct((length, width), F32)] * 2,
            in_specs=[VMEM] * 8,
            out_specs=[VMEM] * 2,
            scratch_shapes=[
                pltpu.VMEM((length, 128), BF16),
                pltpu.VMEM((length, 128), BF16),
                pltpu.VMEM((length, 128), BF16),
                pltpu.VMEM((length, 2 * CHUNK), BF16),
                pltpu.VMEM((128, 128), BF16),
            ],
            compiler_params=params,
            cost_estimate=cost(2 * length * width * 1024, 16 << 20),
            name="intra",
        )(after, step, logdecay, skip, spread, x, b, c)

    if direct:

        def swap(v, k):
            return lax.ppermute(v, "dp", [(i, i ^ k) for i in range(dp)])

        order = [2, 3, 1] if dp == 4 else [1]
        got = {k: swap(local_parts[k], k) for k in order}
        metas = {0: meta, **{k: swap(meta, k) for k in order}}
        metas = [metas[k] for k in range(dp)]
        resumed = pl.pallas_call(
            functools.partial(resume_kernel, ways=dp, heads=heads),
            out_shape=[piece] * dp,
            in_specs=[VMEM] * (dp + 3),
            out_specs=[VMEM] * dp,
            compiler_params=params,
            cost_estimate=cost(2 * rows * 128 * 128 * dp, 2 << 20),
            name="resume",
        )(
            *metas,
            cache_states.reshape(slots, rows, state),
            decays,
            template,
        )
        sent = {k: swap(resumed[k], k) for k in order}
        y, grow = intra(resumed[0][:8, :])
        final = pl.pallas_call(
            functools.partial(final_kernel, ways=dp, dp_name="dp", heads=heads),
            out_shape=jax.ShapeDtypeStruct((dp, rows, state), BF16),
            in_specs=[VMEM] * (3 * dp),
            out_specs=VMEM,
            compiler_params=params,
            cost_estimate=cost(2 * rows * 128 * 128 * dp, 2 << 20),
            name="final",
        )(local_parts[0], *[got[k] for k in range(1, dp)], *resumed, *metas)
        new_states = final.reshape(dp, heads, chan, state)
        arrived = [resumed[0]] + [sent[k] for k in range(1, dp)]
    else:
        metas = lax.all_gather(meta[0], "dp", axis=0)
        ids = metas[:, heads].astype(jnp.int32)
        resumed = (
            cache_states[ids].astype(F32)
            + slot_decay[ids][:, :, None, None] * template_state.astype(F32)[None]
        ).astype(BF16)
        mine = lax.all_to_all(resumed, "dp", split_axis=0, concat_axis=2, tiled=True)
        arrived = [mine.reshape(rows, state)]
        given = lax.all_to_all(
            local_parts[0].reshape(1, heads, HEAD_SIZE, state),
            "dp",
            split_axis=2,
            concat_axis=0,
            tiled=True,
        )
        new_states = (
            given.astype(F32) + metas[:, :heads, None, None] * resumed.astype(F32)
        ).astype(BF16)
        y, grow = intra(local_parts[0][:8, :])

    block = CHUNK
    mixed = pl.pallas_call(
        functools.partial(norm_kernel, ways=ways, dp_name="dp", heads=heads, block=block),
        out_shape=jax.ShapeDtypeStruct((1, length, width), BF16),
        in_specs=[VMEM] * (ways + 6),
        out_specs=pl.BlockSpec(memory_space=pltpu.HBM),
        scratch_shapes=[
            pltpu.VMEM((heads * HEAD_SIZE, state), BF16),
            pltpu.VMEM((length, width), BF16),
            pltpu.SemaphoreType.DMA((length // block,)),
        ],
        compiler_params=params,
        cost_estimate=cost(2 * length * width * 128, 4 << 20),
        name="norm",
    )(*arrived, alive, offset, y, grow, c, gain)
    return (mixed, new_states)


def solution(mesh):
    return jax.shard_map(
        functools.partial(local, dp=mesh.shape["dp"]),
        mesh=mesh,
        in_specs=(
            P(("groups", "dp"), None, "tensor"),
            P(("groups", "dp"), None, "tensor"),
            P(("groups", "dp"), None, "tensor"),
            P(("groups", "dp"), "tensor", None),
            P("tensor"),
            P("tensor"),
            P("tensor"),
            P("tensor"),
            P("groups", "tensor", "dp", None),
            P("groups", "tensor"),
            P(("groups", "tensor"), "dp", None),
            P(("groups", "dp")),
            P(("groups", "dp")),
            P(("groups", "dp")),
        ),
        out_specs=(P(("groups", "dp"), None, "tensor"), P("groups", "tensor", "dp", None)),
        check_vma=False,
    )
```

```python
import functools

import jax
import jax.numpy as jnp
from jax import lax
from jax.experimental import pallas as pl
from jax.experimental.pallas import tpu as pltpu
from jax.sharding import PartitionSpec as P

HEAD_SIZE = 64
GROUP_HEADS = 32
CHUNK = 128
SPAN = 256
LANES = 256
F32 = jnp.float32
BF16 = jnp.bfloat16
VMEM = pl.BlockSpec(memory_space=pltpu.VMEM)
HBM = pl.BlockSpec(memory_space=pltpu.HBM)


def split3(v):
    hi = v.astype(BF16).astype(F32)
    mid = (v - hi).astype(BF16).astype(F32)
    return hi, mid, v - hi - mid


def column(row, heads):
    eye = lax.broadcasted_iota(jnp.int32, (heads, heads), 0) == lax.broadcasted_iota(
        jnp.int32, (heads, heads), 1
    )
    return jnp.sum(jnp.where(eye, row, 0.0), axis=1, keepdims=True)


def turned(v):
    heads, length = v.shape
    return jnp.concatenate([v, jnp.zeros((128 - heads, length), F32)], axis=0).T


def spread(v, first, lanes):
    per = 128 // HEAD_SIZE
    lane = lax.broadcasted_iota(jnp.int32, v.shape, 1)
    tiles = []
    for j in range(lanes // 128):
        head = first + j * per + lax.shift_right_logical(lane, HEAD_SIZE.bit_length() - 1)
        tiles.append(jnp.take_along_axis(v, head, axis=1))
    return jnp.concatenate(tiles, axis=1)


def scan_steps(raw, bias_row, decay_row, alive_count):
    heads, length = raw.shape
    bias = column(bias_row, heads)
    rate = -jnp.exp(column(decay_row, heads))
    position = lax.broadcasted_iota(jnp.int32, (heads, length), 1)
    raw = raw + bias
    soft = jnp.maximum(raw, 0.0) + jnp.log1p(jnp.exp(-jnp.abs(raw)))
    step = jnp.where(position < alive_count, soft, 0.0)
    drop = rate * step
    upper = (
        lax.broadcasted_iota(jnp.int32, (CHUNK, CHUNK), 0)
        <= lax.broadcasted_iota(jnp.int32, (CHUNK, CHUNK), 1)
    )
    upper = jnp.where(upper, 1.0, 0.0).astype(BF16)
    chunks = length // CHUNK
    terms = [t for c in range(chunks) for t in split3(drop[:, c * CHUNK : (c + 1) * CHUNK])]
    sums = jnp.dot(
        jnp.concatenate(terms, axis=0).astype(BF16), upper, preferred_element_type=F32
    )
    base = jnp.zeros((heads, 1), F32)
    parts = []
    for c in range(chunks):
        i = 3 * c * heads
        run = sums[i : i + heads] + sums[i + heads : i + 2 * heads] + sums[i + 2 * heads : i + 3 * heads]
        parts.append(run + base)
        base = base + run[:, CHUNK - 1 :]
    return step, jnp.concatenate(parts, axis=1)


def state_kernel(*refs, ways, dp_name):
    sources, refs = refs[:12], refs[12:]
    pieces, refs = refs[:ways], refs[ways:]
    meta_ref, step_ref, log_ref, b_ref, x_ref, c_ref, skip_ref, gain_ref, template_ref, decays_ref = refs[:10]
    raw_ref, bias_ref, decay_ref, count_ref, hold, sems = refs[10:]
    heads, length = raw_ref.shape
    width = heads * HEAD_SIZE
    chan = HEAD_SIZE // ways
    targets = [raw_ref, bias_ref, decay_ref, count_ref.at[0:1], count_ref.at[1:2], b_ref, x_ref]
    targets += [c_ref, skip_ref, gain_ref, template_ref, decays_ref]
    copies = [
        pltpu.make_async_copy(source, target, sems.at[i])
        for i, (source, target) in enumerate(zip(sources, targets))
    ]
    for copy in copies:
        copy.start()
    for copy in copies[:5]:
        copy.wait()
    step, logdecay = scan_steps(raw_ref[...], bias_ref[...], decay_ref[...], count_ref[0:1, 0:1])
    step_ref[...] = step
    log_ref[...] = logdecay
    end = logdecay[:, length - 1 :]
    tail = turned(jnp.exp(end - logdecay) * step)
    for copy in copies[5:7]:
        copy.wait()
    turned_b = b_ref[...].T
    per = LANES // HEAD_SIZE
    for t in range(width // LANES):
        at = slice(t * LANES, (t + 1) * LANES)
        moved = (spread(tail, t * per, LANES) * x_ref[:, at].astype(F32)).astype(BF16)
        state = jnp.dot(turned_b, moved, preferred_element_type=F32)
        back = state.T.astype(BF16).reshape(per, ways, chan, 128)
        for d in range(ways):
            hold[d, t * per * chan : (t + 1) * per * chan, :] = back[:, d].reshape(per * chan, 128)
    if ways == 1:
        pieces[0][...] = hold[0]
    else:
        me = lax.axis_index(dp_name)
        for k in range(ways):
            pieces[k][...] = hold[me ^ k]
    lane = lax.broadcasted_iota(jnp.int32, (8, 128), 1)
    eye = lax.broadcasted_iota(jnp.int32, (heads, 128), 0) == lax.broadcasted_iota(
        jnp.int32, (heads, 128), 1
    )
    last = jnp.sum(jnp.where(eye, jnp.exp(end), 0.0), axis=0, keepdims=True)
    last = jnp.broadcast_to(last, (8, 128))
    counts = count_ref[...].astype(F32)
    last = jnp.where(lane == heads, counts[1:2, 0:1], last)
    meta_ref[...] = jnp.where(lane == heads + 1, counts[0:1, 0:1], last)
    for copy in copies[7:]:
        copy.wait()


def row_spread(row, heads, rows):
    terms = jnp.concatenate(split3(row) + (jnp.zeros((1, 128 - 3 * heads), F32),), axis=1)
    lanes = jnp.broadcast_to(terms, (128, 128)).astype(BF16)
    at = lax.broadcasted_iota(jnp.int32, (rows, 128), 0) // (rows // heads)
    term = lax.broadcasted_iota(jnp.int32, (rows, 128), 1)
    pick = jnp.where((term % heads == at) & (term < 3 * heads), 1.0, 0.0).astype(BF16)
    return lax.dot_general(pick, lanes, (((1,), (1,)), ((), ())), preferred_element_type=F32)


def resume_kernel(*refs, ways, heads):
    metas, cache_ref, decay_ref, template_ref = refs[:ways], *refs[ways : ways + 3]
    outs = refs[ways + 3 :]
    rows = template_ref.shape[0]
    lane = lax.broadcasted_iota(jnp.int32, (8, 128), 1)
    template = template_ref[...].astype(F32)
    for k in range(ways):
        slot = jnp.max(jnp.where(lane == heads, metas[k][...], 0.0)).astype(jnp.int32)
        factor = row_spread(decay_ref[pl.ds(slot, 1), :], heads, rows)
        outs[k][...] = (cache_ref[slot].astype(F32) + factor * template).astype(BF16)


def intra_kernel(
    after_ref, step_ref, log_ref, skip_ref, x_ref, b_ref, c_ref, y_ref, grow_ref, mix_ref
):
    heads, length = step_ref.shape
    width = heads * HEAD_SIZE
    spans = length // SPAN
    causal = lax.broadcasted_iota(jnp.int32, (SPAN, SPAN), 0) >= lax.broadcasted_iota(
        jnp.int32, (SPAN, SPAN), 1
    )
    lane = lax.broadcasted_iota(jnp.int32, (heads, 128), 1)
    rates = jnp.zeros((heads, 128), F32)
    start = jnp.zeros((heads, 1), F32)
    inner, outer, turned_b = [], [], []
    for i in range(spans):
        at = slice(i * SPAN, (i + 1) * SPAN)
        logdecay = log_ref[:, at]
        middle = logdecay[:, SPAN // 2 - 1 : SPAN // 2]
        end = logdecay[:, SPAN - 1 :]
        inside = logdecay - middle
        inner.append(turned(jnp.exp(-inside) * step_ref[:, at]))
        outer.append(turned(jnp.exp(inside)))
        for j, v in enumerate((jnp.exp(middle - start), jnp.exp(end - middle), jnp.exp(middle))):
            rates = jnp.where(lane == 3 * i + j, v, rates)
        start = end
        gram = lax.dot_general(
            c_ref[at, :], b_ref[at, :], (((1,), (1,)), ((), ())), preferred_element_type=F32
        )
        mix_ref[at, :] = jnp.where(causal, gram, 0.0).astype(BF16)
        turned_b.append(b_ref[at, :].T)
    rates = turned(rates)[: 8 * -(-3 * spans // 8)]
    eight = jnp.broadcast_to(
        jnp.concatenate([skip_ref[...], jnp.zeros((1, 128 - heads), F32)], axis=1), (8, 128)
    )

    per = LANES // HEAD_SIZE
    for t in range(width // LANES):
        at = slice(t * LANES, (t + 1) * LANES)
        skip = spread(eight, t * per, LANES)[0:1]
        rate = spread(rates, t * per, LANES)
        state = None
        for i in range(spans):
            rows = slice(i * SPAN, (i + 1) * SPAN)
            into, out, whole = (rate[3 * i + j : 3 * i + j + 1] for j in range(3))
            x = x_ref[rows, at].astype(F32)
            moved = (x * spread(inner[i], t * per, LANES)).astype(BF16)
            mixed = jnp.dot(mix_ref[rows, :], moved, preferred_element_type=F32)
            if state is not None:
                mixed += jnp.dot(
                    c_ref[rows, :], (into * state).astype(BF16), preferred_element_type=F32
                )
            scale = spread(outer[i], t * per, LANES)
            y_ref[rows, at] = scale * mixed + skip * x
            grow_ref[rows, at] = scale * whole
            if i + 1 < spans:
                fresh = jnp.dot(turned_b[i], moved, preferred_element_type=F32)
                state = out * (fresh if state is None else into * state + fresh)


def norm_kernel(*refs, ways, dp_name, heads, block):
    pieces, refs = refs[:ways], refs[ways:]
    meta_ref, offset_ref, y_ref, grow_ref, c_ref, gain_ref, mixed_ref, hold, scan_ref, done, sems = refs
    chan = HEAD_SIZE // ways
    width = heads * HEAD_SIZE
    if ways == 1:
        hold[...] = pieces[0][...]
    else:
        me = lax.axis_index(dp_name)
        for k in range(ways):
            start = pl.multiple_of((me ^ k) * chan, chan)
            for h in range(heads):
                hold[pl.ds(h * HEAD_SIZE + start, chan), :] = pieces[k][h * chan : (h + 1) * chan, :]
    position = lax.broadcasted_iota(jnp.int32, (block, 1), 0).astype(F32)
    length, offset = meta_ref[0:1, heads + 1 : heads + 2], offset_ref[...].astype(F32)
    copies = []
    for i in range(y_ref.shape[0] // block):
        rows = slice(i * block, (i + 1) * block)
        squares = jnp.zeros((block, 128), F32)
        for t in range(width // LANES):
            at = slice(t * LANES, (t + 1) * LANES)
            carried = lax.dot_general(
                c_ref[rows, :], hold[at, :], (((1,), (1,)), ((), ())), preferred_element_type=F32
            )
            scan = y_ref[rows, at] + grow_ref[rows, at] * carried
            scan_ref[rows, at] = scan
            for j in range(LANES // 128):
                part = scan[:, j * 128 : (j + 1) * 128]
                squares += part * part
        meansq = jnp.sum(squares, axis=1, keepdims=True) * (1.0 / width)
        keep = (position + i * block < length) & (position + i * block >= offset)
        factor = jnp.where(keep, lax.rsqrt(meansq + 1e-05), 0.0)
        for t in range(width // LANES):
            at = slice(t * LANES, (t + 1) * LANES)
            done[rows, at] = (scan_ref[rows, at] * factor * gain_ref[:, at]).astype(BF16)
        copy = pltpu.make_async_copy(done.at[rows, :], mixed_ref.at[0, rows, :], sems.at[i])
        copy.start()
        copies.append(copy)
    for copy in copies:
        copy.wait()


def final_kernel(*refs, ways, dp_name, heads):
    pieces, resumed, metas = refs[:ways], refs[ways : 2 * ways], refs[2 * ways : 3 * ways]
    out_ref = refs[3 * ways]
    rows = pieces[0].shape[0]
    me = lax.axis_index(dp_name)
    for k in range(ways):
        whole = row_spread(metas[k][0:1, :heads], heads, rows)
        out_ref[me ^ k] = (
            pieces[k][...].astype(F32) + whole * resumed[k][...].astype(F32)
        ).astype(BF16)


def pinned(v):
    return v if v.dtype == jnp.int32 else pltpu.with_memory_space_constraint(v, pltpu.HBM)


def cost(flops, size):
    return pl.CostEstimate(flops=flops, bytes_accessed=size, transcendentals=0)


def local(
    ssm_input,
    input_proj,
    output_proj,
    step_raw,
    step_bias,
    decay_log,
    skip_gain,
    norm_gain,
    cache_states,
    slot_decay,
    template_state,
    slot_ids,
    row_lengths,
    row_offsets,
    *,
    dp,
):
    _, length, width = ssm_input.shape
    heads = step_raw.shape[1]
    slots, _, chan, state = cache_states.shape
    direct = dp in (2, 4)
    ways = dp if direct else 1
    rows = heads * HEAD_SIZE // ways
    piece = jax.ShapeDtypeStruct((rows, state), BF16)
    params = pltpu.CompilerParams(vmem_limit_bytes=24 << 20)
    loaded = [
        step_raw[0],
        step_bias[None],
        decay_log[None],
        row_lengths[None],
        slot_ids[None],
        input_proj[0],
        ssm_input[0],
        output_proj[0],
        skip_gain[None],
        norm_gain[None],
        template_state.reshape(-1, state),
        slot_decay,
    ]
    like = lambda v: jax.ShapeDtypeStruct(v.shape, v.dtype)
    outs = pl.pallas_call(
        functools.partial(state_kernel, ways=ways, dp_name="dp"),
        out_shape=[piece] * ways
        + [jax.ShapeDtypeStruct((8, 128), F32)]
        + [jax.ShapeDtypeStruct((heads, length), F32)] * 2
        + [like(v) for v in loaded[5:]],
        in_specs=[HBM] * len(loaded),
        out_specs=[VMEM] * (ways + 3 + len(loaded[5:])),
        scratch_shapes=[
            pltpu.VMEM((heads, length), F32),
            pltpu.VMEM((1, heads), F32),
            pltpu.VMEM((1, heads), F32),
            pltpu.VMEM((2, 1), jnp.int32),
            pltpu.VMEM((ways, rows, state), BF16),
            pltpu.SemaphoreType.DMA((len(loaded),)),
        ],
        compiler_params=params,
        cost_estimate=cost(2 * length * width * 256, 3 << 20),
        name="state",
    )(*[pinned(v) for v in loaded])
    local_parts = outs[:ways]
    meta, step, logdecay, b, x, c, skip, gain, template, decays = outs[ways:]

    def intra(after):
        return pl.pallas_call(
            intra_kernel,
            out_shape=[jax.ShapeDtypeStruct((length, width), F32)] * 2,
            in_specs=[VMEM] * 7,
            out_specs=[VMEM] * 2,
            scratch_shapes=[pltpu.VMEM((length, SPAN), BF16)],
            compiler_params=params,
            cost_estimate=cost(2 * length * width * 1024, 16 << 20),
            name="intra",
        )(after, step, logdecay, skip, x, b, c)

    if direct:

        def swap(v, k):
            return lax.ppermute(v, "dp", [(i, i ^ k) for i in range(dp)])

        order = [2, 3, 1] if dp == 4 else [1]
        got = {k: swap(local_parts[k], k) for k in order}
        metas = {0: meta, **{k: swap(meta, k) for k in order}}
        metas = [metas[k] for k in range(dp)]
        resumed = pl.pallas_call(
            functools.partial(resume_kernel, ways=dp, heads=heads),
            out_shape=[piece] * dp,
            in_specs=[VMEM] * (dp + 3),
            out_specs=[VMEM] * dp,
            compiler_params=params,
            cost_estimate=cost(2 * rows * 128 * 128 * dp, 2 << 20),
            name="resume",
        )(
            *metas,
            cache_states.reshape(slots, rows, state),
            decays,
            template,
        )
        sent = {k: swap(resumed[k], k) for k in order}
        y, grow = intra(resumed[0][:8, :])
        final = pl.pallas_call(
            functools.partial(final_kernel, ways=dp, dp_name="dp", heads=heads),
            out_shape=jax.ShapeDtypeStruct((dp, rows, state), BF16),
            in_specs=[VMEM] * (3 * dp),
            out_specs=VMEM,
            compiler_params=params,
            cost_estimate=cost(2 * rows * 128 * 128 * dp, 2 << 20),
            name="final",
        )(local_parts[0], *[got[k] for k in range(1, dp)], *resumed, *metas)
        new_states = final.reshape(dp, heads, chan, state)
        arrived = [resumed[0]] + [sent[k] for k in range(1, dp)]
    else:
        metas = lax.all_gather(meta[0], "dp", axis=0)
        ids = metas[:, heads].astype(jnp.int32)
        resumed = (
            cache_states[ids].astype(F32)
            + slot_decay[ids][:, :, None, None] * template_state.astype(F32)[None]
        ).astype(BF16)
        mine = lax.all_to_all(resumed, "dp", split_axis=0, concat_axis=2, tiled=True)
        arrived = [mine.reshape(rows, state)]
        given = lax.all_to_all(
            local_parts[0].reshape(1, heads, HEAD_SIZE, state),
            "dp",
            split_axis=2,
            concat_axis=0,
            tiled=True,
        )
        new_states = (
            given.astype(F32) + metas[:, :heads, None, None] * resumed.astype(F32)
        ).astype(BF16)
        y, grow = intra(local_parts[0][:8, :])

    block = CHUNK
    mixed = pl.pallas_call(
        functools.partial(norm_kernel, ways=ways, dp_name="dp", heads=heads, block=block),
        out_shape=jax.ShapeDtypeStruct((1, length, width), BF16),
        in_specs=[VMEM] * (ways + 6),
        out_specs=HBM,
        scratch_shapes=[
            pltpu.VMEM((heads * HEAD_SIZE, state), BF16),
            pltpu.VMEM((length, width), F32),
            pltpu.VMEM((length, width), BF16),
            pltpu.SemaphoreType.DMA((length // block,)),
        ],
        compiler_params=params,
        cost_estimate=cost(2 * length * width * 128, 4 << 20),
        name="norm",
    )(*arrived, meta, row_offsets[None], y, grow, c, gain)
    return (mixed, new_states)


def solution(mesh):
    return jax.shard_map(
        functools.partial(local, dp=mesh.shape["dp"]),
        mesh=mesh,
        in_specs=(
            P(("groups", "dp"), None, "tensor"),
            P(("groups", "dp"), None, "tensor"),
            P(("groups", "dp"), None, "tensor"),
            P(("groups", "dp"), "tensor", None),
            P("tensor"),
            P("tensor"),
            P("tensor"),
            P("tensor"),
            P("groups", "tensor", "dp", None),
            P("groups", "tensor"),
            P(("groups", "tensor"), "dp", None),
            P(("groups", "dp")),
            P(("groups", "dp")),
            P(("groups", "dp")),
        ),
        out_specs=(P(("groups", "dp"), None, "tensor"), P("groups", "tensor", "dp", None)),
        check_vma=False,
    )
```
